32 devices in a mesh: batch: 4 (over y, x), ctx: 8 (over z, core).
Axes of the slice: x: 2, y: 2, z: 4, core: 2. Of those that a mesh axis runs over, the one named last changes fastest.
Arguments:
- inputs: bfloat16 [4, 1024, 1024], P('batch', 'ctx'), may hold values from -6 to 6
- segments: int32 [4, 1024], P('batch', 'ctx'), may hold values from 0 to 3, never falling along the last dimension, each value on 1 to 512 neighbouring positions
- routes: int32 [4, 1024, 8], P('batch', 'ctx'), may hold values from 0 to 31, all different within a row; in each aligned block of 128 rows (0 to 127, 128 to 255, ..., all dimensions but the last counted through in order) at most 48 rows name the same one
- cotangent: bfloat16 [4, 1024, 1024], P('batch', 'ctx'), may hold values from -6 to 6
- w_query: bfloat16 [1024, 1024], P(('batch', 'ctx')), may hold values from -0.1875 to 0.1875
- w_key: bfloat16 [1024, 512], P(('batch', 'ctx')), may hold values from -0.1875 to 0.1875
- w_value: bfloat16 [1024, 512], P(('batch', 'ctx')), may hold values from -0.1875 to 0.1875
- w_output: bfloat16 [1024, 1024], P(('batch', 'ctx')), may hold values from -0.75 to 0.75
- w_router: bfloat16 [1024, 32], P(('batch', 'ctx')), may hold values from -0.5 to 0.5
- norm_attn: bfloat16 [1024], P(('batch', 'ctx')), may hold values from 0.5 to 1.5
- norm_moe: bfloat16 [1024], P(('batch', 'ctx')), may hold values from 0.5 to 1.5
- w_gate: bfloat16 [32, 1024, 512], P('ctx', 'batch'), may hold values from -0.1875 to 0.1875
- w_up: bfloat16 [32, 1024, 512], P('ctx', 'batch'), may hold values from -0.1875 to 0.1875
- w_down: bfloat16 [32, 1024, 512], P('ctx', 'batch'), may hold values from -0.25 to 0.25
Outputs:
- block_out: bfloat16 [4, 1024, 1024], P('batch', 'ctx')
- grad_inputs: float32 [4, 1024, 1024], P('batch', 'ctx')
- grad_w_query: float32 [1024, 1024], P(('batch', 'ctx'))
- grad_w_key: float32 [1024, 512], P(('batch', 'ctx'))
- grad_w_value: float32 [1024, 512], P(('batch', 'ctx'))
- grad_w_output: float32 [1024, 1024], P(('batch', 'ctx'))
- grad_w_router: float32 [1024, 32], P(('batch', 'ctx'))
- grad_norm_attn: float32 [1024], P(('batch', 'ctx'))
- grad_norm_moe: float32 [1024], P(('batch', 'ctx'))
- grad_w_gate: float32 [32, 1024, 512], P('ctx', 'batch')
- grad_w_up: float32 [32, 1024, 512], P('ctx', 'batch')
- grad_w_down: float32 [32, 1024, 512], P('ctx', 'batch')
The draws below stay inside these ranges and needn't reach their ends.
Inputs may be any that keep to these rules, and one draw needn't show every extreme that they name: `routes`: each token names 8 different experts. Among the 128 tokens of one device (aligned blocks of the token order), no expert is named more than 48 times, and in some blocks some expert exactly 48 times. `segments`: documents are numbered from 0 along each sequence, never falling; a document has at most half of 1024 tokens, and some document is exactly that long.
All inputs are finite; a program needn't handle non-finite values.
Results may differ from the reference program's by a relative error of at most 0.018.
Values may be sent and summed in bfloat16 or wider, within the bound.
A program may use at most 192 MiB of HBM per device.

```python
import math
import jax
import jax.numpy as jnp
import numpy as np
from jax import lax

D = 1024
HEADS = 16
KV_HEADS = 8
HEAD_DIM = 64
EXPERTS = 32
FF_E = 512
TOPK = 8
TOK_DEV = 128
LENGTH = 1024
SEQS = 4
CAP = 48
N_CTX = 8


def level_of(rng, dims, pieces, smallest, largest):
    def one(axis_at, shards_of):
        steps = jax.random.uniform(jax.random.fold_in(jax.random.fold_in(rng, 6), axis_at), (shards_of,), jnp.float32, smallest / len(pieces), largest / len(pieces))
        return jnp.repeat(jnp.exp(steps), dims[axis_at] // shards_of).reshape((-1,) + (1,) * (len(dims) - axis_at - 1))

    loudness = one(*pieces[0])
    for cut in pieces[1:]:
        loudness = loudness * one(*cut)
    return loudness


def split_up(count, total, limit, skew):
    portions = [(1 << 20) // math.isqrt(grade ** skew) + 1 for grade in range(2, count + 1)]
    surplus, counts = total - limit - (count - 1), [1] * (count - 1)
    while surplus > 0:
        candidates = [i for i in range(count - 1) if counts[i] < limit]
        pool, remaining = sum([portions[i] for i in candidates]), surplus
        for i in candidates:
            more = min(limit - counts[i], max(1, remaining * portions[i] // pool), surplus)
            counts[i] = counts[i] + more
            surplus = surplus - more
    return np.array([limit] + counts)


def ragged(rng, amount, total, reach, slope):
    if amount == 2:
        one = jax.random.randint(rng, (), max(1, total - reach), min(reach, total - 1) + 1)
        return jnp.stack([one, total - one])
    sizes = jnp.asarray(split_up(amount, total, reach, slope), jnp.int32)
    twos = (amount - 1) // 2
    source_of, taker = sizes[1:1 + 2 * twos:2], sizes[2:2 + 2 * twos:2]
    slack = jnp.minimum(source_of - 1, reach - taker)
    passed = jax.random.randint(jax.random.fold_in(rng, 1), (twos,), 0, 1 << 20) % (slack + 1)
    sizes = sizes.at[1:1 + 2 * twos:2].set(source_of - passed).at[2:2 + 2 * twos:2].set(taker + passed)
    return sizes[jax.random.permutation(jax.random.fold_in(rng, 2), amount)]


def assign_block(key, own, number, rows, amount, top, limit, lean):
    ranking = jax.random.permutation(key, amount)
    packed, common = portions_of(amount, rows * top, limit, lean, True), portions_of(amount, rows * top, limit, lean, False)
    places = jnp.arange(amount)

    def named(tallies, turn):
        used = int((tallies > 0).sum())
        fixed = max(1, used // 4)
        passed = fixed + (places - fixed + turn * (used - fixed)) % max(1, amount - fixed)
        return jnp.zeros((amount,), jnp.int32).at[ranking[jnp.where(places < fixed, places, passed)]].set(jnp.asarray(tallies, jnp.int32))

    tallies = jnp.where(number % 4 == 0, named(packed, number // 4), named(common, number - number // 4 - 1))
    mixed = jax.random.permutation(jax.random.fold_in(own, 3), amount)
    giver, receiver = mixed[0:amount // 2 * 2:2], mixed[1:amount // 2 * 2:2]
    slack = jnp.minimum(tallies[giver] - 1, limit - tallies[receiver]) // 2
    slack = jnp.where((giver == ranking[0]) | (receiver == ranking[0]) | (tallies[receiver] == 0), 0, jnp.maximum(slack, 0))
    passed = jax.random.randint(jax.random.fold_in(own, 4), (amount // 2,), 0, 1 << 20) % (slack + 1)
    tallies = tallies.at[giver].add(-passed).at[receiver].add(passed)
    labels = jnp.searchsorted(jnp.cumsum(tallies), jnp.arange(rows * top), side="right").astype(jnp.int32)
    listing = labels.reshape(top, rows).T
    listing = listing[jax.random.permutation(jax.random.fold_in(own, 1), rows)]
    turn = jax.random.randint(jax.random.fold_in(own, 2), (rows, 1), 0, top)
    return jnp.take_along_axis(listing, (jnp.arange(top)[None, :] + turn) % top, axis=1)


def portions_of(count, total, bound, slope, full):
    weights = [(1 << 20) // math.isqrt(grade ** slope) + 1 for grade in range(1, count + 1)]
    largest = bound if full else min(bound, max(-(-total // count), total * weights[0] // sum(weights)))
    least = 1 if total - largest >= count - 1 else 0
    given, surplus = [largest] + [least] * (count - 1), total - largest - least * (count - 1)
    while surplus > 0:
        movable = [i for i in range(1, count) if given[i] < largest] or [i for i in range(1, count) if given[i] < bound]
        pool, remaining = sum([weights[i] for i in movable]), surplus
        for i in movable:
            extra = min(bound - given[i], max(1, remaining * weights[i] // pool), surplus)
            given[i] = given[i] + extra
            surplus = surplus - extra
    return np.array(given)


def scatter_about(key, dims, scale, reach, pieces=(), kind=jnp.bfloat16):
    values = scale * jax.random.normal(key, dims, jnp.float32)
    if pieces:
        values = values * level_of(key, dims, pieces, -0.22, 0.18)
    return jnp.clip(values, -reach, reach).astype(kind)


def setup_inputs(seed: int = 0) -> dict:
    key_list = jax.random.split(jax.random.key(seed), 15)
    inputs = scatter_about(key_list[0], (SEQS, LENGTH, D), 1.0, 6.0, ((0, 4), (1, 8)))
    segments = jax.vmap(lambda own: jnp.searchsorted(jnp.cumsum(ragged(own, 4, LENGTH, LENGTH // 2, 1)), jnp.arange(LENGTH), side="right"))(jax.random.split(key_list[1], SEQS)).reshape((SEQS, LENGTH)).astype(jnp.int32)
    routes_keys = jax.random.split(jax.random.fold_in(key_list[2], 1), SEQS * LENGTH // TOK_DEV)
    routes_turns = jax.random.permutation(jax.random.fold_in(key_list[2], 3), SEQS * LENGTH // TOK_DEV)
    routes = jax.vmap(lambda own, number: assign_block(jax.random.fold_in(key_list[2], 2), own, number, TOK_DEV, EXPERTS, TOPK, CAP, 1))(routes_keys, routes_turns).reshape((SEQS, LENGTH, TOPK))
    cotangent = scatter_about(key_list[3], (SEQS, LENGTH, D), 1.0, 6.0, ((0, 4), (1, 8)))
    w_query = scatter_about(key_list[4], (D, HEADS * HEAD_DIM), D ** -0.5, 0.1875, ((0, 32),))
    w_key = scatter_about(key_list[5], (D, KV_HEADS * HEAD_DIM), D ** -0.5, 0.1875, ((0, 32),))
    w_value = scatter_about(key_list[6], (D, KV_HEADS * HEAD_DIM), D ** -0.5, 0.1875, ((0, 32),))
    w_output = scatter_about(key_list[7], (HEADS * HEAD_DIM, D), (D // 16) ** -0.5, 0.75, ((0, 32),))
    w_router = scatter_about(key_list[8], (D, EXPERTS), (D // 9) ** -0.5, 0.5, ((0, 32),))
    norm_attn = jnp.clip(1.0 + 0.1 * jax.random.normal(key_list[9], (D,), jnp.float32), 0.5, 1.5).astype(jnp.bfloat16)
    norm_moe = jnp.clip(1.0 + 0.1 * jax.random.normal(key_list[10], (D,), jnp.float32), 0.5, 1.5).astype(jnp.bfloat16)
    w_gate = scatter_about(key_list[11], (EXPERTS, D, FF_E), D ** -0.5, 0.1875, ((0, 8), (1, 4)))
    w_up = scatter_about(key_list[12], (EXPERTS, D, FF_E), D ** -0.5, 0.1875, ((0, 8), (1, 4)))
    w_down = scatter_about(key_list[13], (EXPERTS, D, FF_E), FF_E ** -0.5, 0.25, ((0, 8), (1, 4)))
    return {"inputs": inputs, "segments": segments, "routes": routes, "cotangent": cotangent, "w_query": w_query, "w_key": w_key, "w_value": w_value, "w_output": w_output, "w_router": w_router, "norm_attn": norm_attn, "norm_moe": norm_moe, "w_gate": w_gate, "w_up": w_up, "w_down": w_down}


EPS = 1e-06
ROPE_BASE = 10000.0

def rounded(value):
    return lax.optimization_barrier(value.astype(jnp.bfloat16)).astype(jnp.float32)

def rope_tables(positions, head_size):
    half_size = head_size // 2
    exponent = jnp.arange(half_size, dtype=jnp.float32) * (2.0 / head_size)
    inverse = jnp.exp(-exponent * math.log(ROPE_BASE))
    angles = positions.astype(jnp.float32)[:, None] * inverse[None, :]
    return (jnp.cos(angles), jnp.sin(angles))

def rotate(values, cos_table, sin_table):
    half_size = values.shape[-1] // 2
    lower_half = values[..., :half_size]
    upper_half = values[..., half_size:]
    cos_part = cos_table[:, None, :]
    sin_part = sin_table[:, None, :]
    return jnp.concatenate([lower_half * cos_part - upper_half * sin_part, upper_half * cos_part + lower_half * sin_part], axis=-1)

def route_slots(route_ids, experts, capacity):
    flat_ids = route_ids.reshape(-1)
    chosen = (flat_ids[:, None] == jnp.arange(experts, dtype=jnp.int32)[None, :]).astype(jnp.int32)
    earlier = jnp.cumsum(chosen, axis=0) - chosen
    return (flat_ids * capacity + lax.optimization_barrier(jnp.sum(earlier * chosen, axis=1))).astype(jnp.int32)

def attend(queries, key_rows, value_rows, allowed, score_scale):
    scores = jnp.einsum('tkgd,skd->kgts', queries.astype(jnp.float32), key_rows.astype(jnp.float32)) * score_scale
    exp_scores = jnp.where(allowed[None, None], jnp.exp(scores), 0.0)
    totals = lax.optimization_barrier(jnp.sum(exp_scores, axis=-1, keepdims=True))
    prob_wire = rounded(exp_scores / totals)
    output = jnp.einsum('kgts,skd->tkgd', prob_wire, value_rows.astype(jnp.float32))
    return (output.astype(jnp.bfloat16), jnp.log(totals))

def attend_back(queries, key_rows, value_rows, allowed, score_scale, log_totals, attn_rows, grad_rows):
    query_wide = queries.astype(jnp.float32)
    key_wide = key_rows.astype(jnp.float32)
    grad_wide = grad_rows.astype(jnp.float32)
    scores = jnp.einsum('tkgd,skd->kgts', query_wide, key_wide) * score_scale
    prob_again = jnp.where(allowed[None, None], jnp.exp(scores - log_totals), 0.0)
    prob_wire = rounded(prob_again)
    delta_rows = lax.optimization_barrier(jnp.sum(grad_wide * attn_rows.astype(jnp.float32), axis=-1))
    grad_prob = jnp.einsum('tkgd,skd->kgts', grad_wide, value_rows.astype(jnp.float32))
    grad_score = rounded(prob_again * (grad_prob - jnp.transpose(delta_rows, (1, 2, 0))[..., None]) * score_scale)
    grad_queries = jnp.einsum('kgts,skd->tkgd', grad_score, key_wide)
    grad_keys = jnp.einsum('kgts,tkgd->skd', grad_score, query_wide)
    grad_values = jnp.einsum('kgts,tkgd->skd', prob_wire, grad_wide)
    return (grad_queries, grad_keys, grad_values)

def reference(inputs, segments, routes, cotangent, w_query, w_key, w_value, w_output, w_router, norm_attn, norm_moe, w_gate, w_up, w_down):
    score_scale = 1.0 / math.sqrt(HEAD_DIM)
    groups_per = HEADS // KV_HEADS
    positions = jnp.arange(LENGTH, dtype=jnp.int32)
    cos_table, sin_table = rope_tables(positions, HEAD_DIM)
    gain_attn = norm_attn.astype(jnp.float32)
    gain_moe = norm_moe.astype(jnp.float32)
    gate_wide = w_gate.astype(jnp.float32)
    up_wide = w_up.astype(jnp.float32)
    down_wide = w_down.astype(jnp.float32)
    expert_ids = jnp.arange(EXPERTS, dtype=jnp.int32)

    def one_sequence(sums, seq_args):
        seq_inputs, seq_segments, seq_routes, seq_cotangent = seq_args
        residual_in = seq_inputs.astype(jnp.float32)
        inv_first = lax.rsqrt(lax.optimization_barrier(jnp.mean(residual_in * residual_in, axis=-1, keepdims=True)) + EPS)
        normed_attn = (residual_in * inv_first * gain_attn).astype(jnp.bfloat16)
        query_proj = jnp.dot(normed_attn, w_query, preferred_element_type=jnp.float32)
        key_proj = jnp.dot(normed_attn, w_key, preferred_element_type=jnp.float32)
        value_proj = jnp.dot(normed_attn, w_value, preferred_element_type=jnp.float32)
        query_rot = rotate(query_proj.reshape(LENGTH, HEADS, HEAD_DIM), cos_table, sin_table).astype(jnp.bfloat16)
        key_rot = rotate(key_proj.reshape(LENGTH, KV_HEADS, HEAD_DIM), cos_table, sin_table).astype(jnp.bfloat16)
        value_heads = value_proj.astype(jnp.bfloat16).reshape(LENGTH, KV_HEADS, HEAD_DIM)
        query_blocks = query_rot.reshape(N_CTX, TOK_DEV, KV_HEADS, groups_per, HEAD_DIM)
        seg_blocks = seq_segments.reshape(N_CTX, TOK_DEV)
        pos_blocks = positions.reshape(N_CTX, TOK_DEV)

        def mask_for(block_seg, block_pos):
            return (block_seg[:, None] == seq_segments[None, :]) & (positions[None, :] <= block_pos[:, None])

        def forward_block(block_args):
            block_query, block_seg, block_pos = block_args
            return attend(block_query, key_rot, value_heads, mask_for(block_seg, block_pos), score_scale)
        attn_blocks, log_blocks = lax.map(forward_block, (query_blocks, seg_blocks, pos_blocks))
        attn_flat = attn_blocks.reshape(LENGTH, HEADS * HEAD_DIM)
        hidden_res = residual_in + jnp.dot(attn_flat, w_output, preferred_element_type=jnp.float32)
        inv_second = lax.rsqrt(lax.optimization_barrier(jnp.mean(hidden_res * hidden_res, axis=-1, keepdims=True)) + EPS)
        normed_moe = (hidden_res * inv_second * gain_moe).astype(jnp.bfloat16)
        logits = jnp.dot(normed_moe, w_router, preferred_element_type=jnp.float32)
        route_hot = (seq_routes[:, :, None] == expert_ids[None, None, :]).astype(jnp.float32)
        chosen_logits = lax.optimization_barrier(jnp.sum(route_hot * logits[:, None, :], axis=-1))
        route_exp = jnp.exp(chosen_logits)
        route_weights = route_exp / lax.optimization_barrier(jnp.sum(route_exp, axis=-1, keepdims=True))
        slot_rows = jax.vmap(lambda block_routes: route_slots(block_routes, EXPERTS, CAP))(seq_routes.reshape(N_CTX, TOK_DEV, TOPK))

        def to_buffers(rows_in):
            blocked = rows_in.reshape(N_CTX, TOK_DEV * TOPK, D)
            empty = jnp.zeros((N_CTX, EXPERTS * CAP, D), jnp.bfloat16)
            filled = jax.vmap(lambda buffer, slot_ids, row_vals: buffer.at[slot_ids].set(row_vals))(empty, slot_rows, blocked)
            return filled.reshape(N_CTX, EXPERTS, CAP, D).transpose(1, 0, 2, 3)

        def from_buffers(buffers):
            flat_back = buffers.transpose(1, 0, 2, 3).reshape(N_CTX, EXPERTS * CAP, D)
            taken = jax.vmap(lambda buffer, slot_ids: buffer[slot_ids])(flat_back, slot_rows)
            return taken.reshape(LENGTH, TOPK, D)
        expert_in = to_buffers(jnp.repeat(normed_moe, TOPK, axis=0))
        expert_wide = expert_in.astype(jnp.float32)
        gate_pre = jnp.einsum('ebcd,edf->ebcf', expert_wide, gate_wide)
        up_pre = jnp.einsum('ebcd,edf->ebcf', expert_wide, up_wide)
        sigmoid_gate = jax.nn.sigmoid(gate_pre)
        silu_gate = gate_pre * sigmoid_gate
        hidden_act = rounded(silu_gate * up_pre)
        expert_out = jnp.einsum('ebcf,edf->ebcd', hidden_act, down_wide).astype(jnp.bfloat16)
        picked = from_buffers(expert_out).astype(jnp.float32)
        moe_out = lax.optimization_barrier(jnp.sum(route_weights[:, :, None] * picked, axis=1))
        block_out = (hidden_res + moe_out).astype(jnp.bfloat16)
        grad_out = seq_cotangent.astype(jnp.float32)
        grad_weights = lax.optimization_barrier(jnp.sum(grad_out[:, None, :] * picked, axis=-1))
        grad_chosen = route_weights * (grad_weights - lax.optimization_barrier(jnp.sum(route_weights * grad_weights, axis=-1, keepdims=True)))
        grad_logits = lax.optimization_barrier(jnp.sum(route_hot * grad_chosen[:, :, None], axis=1)).astype(jnp.bfloat16)
        grad_router = jnp.dot(normed_moe.T, grad_logits, preferred_element_type=jnp.float32)
        grad_normed = jnp.dot(grad_logits, w_router.T, preferred_element_type=jnp.float32)
        grad_slots = (route_weights[:, :, None] * grad_out[:, None, :]).astype(jnp.bfloat16)
        grad_buffers = to_buffers(grad_slots.reshape(LENGTH * TOPK, D))
        grad_wide = grad_buffers.astype(jnp.float32)
        grad_hidden = jnp.einsum('ebcd,edf->ebcf', grad_wide, down_wide)
        grad_gate = rounded(grad_hidden * up_pre * sigmoid_gate * (1.0 + gate_pre * (1.0 - sigmoid_gate)))
        grad_up = rounded(grad_hidden * silu_gate)
        grad_expert_in = (jnp.einsum('ebcf,edf->ebcd', grad_gate, gate_wide) + jnp.einsum('ebcf,edf->ebcd', grad_up, up_wide)).astype(jnp.bfloat16)
        grad_w_gate = jnp.einsum('ebcd,ebcf->edf', expert_wide, grad_gate)
        grad_w_up = jnp.einsum('ebcd,ebcf->edf', expert_wide, grad_up)
        grad_w_down = jnp.einsum('ebcd,ebcf->edf', grad_wide, hidden_act)
        grad_normed = grad_normed + lax.optimization_barrier(jnp.sum(from_buffers(grad_expert_in).astype(jnp.float32), axis=1))
        gained_moe = grad_normed * gain_moe
        grad_gain_moe = lax.optimization_barrier(jnp.sum(grad_normed * hidden_res * inv_second, axis=0))
        grad_hidden_res = grad_out + inv_second * gained_moe - hidden_res * inv_second ** 3 * lax.optimization_barrier(jnp.mean(gained_moe * hidden_res, axis=-1, keepdims=True))
        grad_attn = grad_hidden_res.astype(jnp.bfloat16)
        grad_w_output = jnp.dot(attn_flat.T, grad_attn, preferred_element_type=jnp.float32)
        grad_attn_rows = jnp.dot(grad_attn, w_output.T, preferred_element_type=jnp.float32).astype(jnp.bfloat16)
        grad_attn_blocks = grad_attn_rows.reshape(N_CTX, TOK_DEV, KV_HEADS, groups_per, HEAD_DIM)

        def backward_block(key_sums, block_args):
            block_query, block_seg, block_pos, block_log, block_attn, block_grad = block_args
            grad_query_block, grad_key_block, grad_value_block = attend_back(block_query, key_rot, value_heads, mask_for(block_seg, block_pos), score_scale, block_log, block_attn, block_grad)
            return ((key_sums[0] + grad_key_block, key_sums[1] + grad_value_block), grad_query_block)
        zero_keys = jnp.zeros((LENGTH, KV_HEADS, HEAD_DIM), jnp.float32)
        key_value_sums, grad_query_blocks = lax.scan(backward_block, (zero_keys, zero_keys), (query_blocks, seg_blocks, pos_blocks, log_blocks, attn_blocks, grad_attn_blocks))
        grad_query = rotate(grad_query_blocks.reshape(LENGTH, HEADS, HEAD_DIM), cos_table, -sin_table).reshape(LENGTH, HEADS * HEAD_DIM).astype(jnp.bfloat16)
        grad_key = rotate(key_value_sums[0], cos_table, -sin_table).reshape(LENGTH, KV_HEADS * HEAD_DIM).astype(jnp.bfloat16)
        grad_value = key_value_sums[1].reshape(LENGTH, KV_HEADS * HEAD_DIM).astype(jnp.bfloat16)
        grad_w_query = jnp.dot(normed_attn.T, grad_query, preferred_element_type=jnp.float32)
        grad_w_key = jnp.dot(normed_attn.T, grad_key, preferred_element_type=jnp.float32)
        grad_w_value = jnp.dot(normed_attn.T, grad_value, preferred_element_type=jnp.float32)
        grad_normed_attn = jnp.dot(grad_query, w_query.T, preferred_element_type=jnp.float32) + jnp.dot(grad_key, w_key.T, preferred_element_type=jnp.float32) + jnp.dot(grad_value, w_value.T, preferred_element_type=jnp.float32)
        gained_attn = grad_normed_attn * gain_attn
        grad_gain_attn = lax.optimization_barrier(jnp.sum(grad_normed_attn * residual_in * inv_first, axis=0))
        grad_inputs = grad_hidden_res + inv_first * gained_attn - residual_in * inv_first ** 3 * lax.optimization_barrier(jnp.mean(gained_attn * residual_in, axis=-1, keepdims=True))
        terms = (grad_w_query, grad_w_key, grad_w_value, grad_w_output, grad_router, grad_gain_attn, grad_gain_moe, grad_w_gate, grad_w_up, grad_w_down)
        return (jax.tree.map(jnp.add, sums, terms), (block_out, grad_inputs))
    start_sums = (jnp.zeros((D, HEADS * HEAD_DIM), jnp.float32), jnp.zeros((D, KV_HEADS * HEAD_DIM), jnp.float32), jnp.zeros((D, KV_HEADS * HEAD_DIM), jnp.float32), jnp.zeros((HEADS * HEAD_DIM, D), jnp.float32), jnp.zeros((D, EXPERTS), jnp.float32), jnp.zeros((D,), jnp.float32), jnp.zeros((D,), jnp.float32), jnp.zeros((EXPERTS, D, FF_E), jnp.float32), jnp.zeros((EXPERTS, D, FF_E), jnp.float32), jnp.zeros((EXPERTS, D, FF_E), jnp.float32))
    sums, outputs = lax.scan(one_sequence, start_sums, (inputs, segments, routes, cotangent))
    return (outputs[0], outputs[1], sums[0], sums[1], sums[2], sums[3], sums[4], sums[5], sums[6], sums[7], sums[8], sums[9])
```

```python
import math

import jax
import jax.numpy as jnp
from jax import lax
from jax.sharding import PartitionSpec as P

HEADS = 16
KV_HEADS = 8
HEAD_DIM = 64
CAP = 48


EPS = 1e-06
ROPE_BASE = 10000.0


def rope_tables(positions, head_size):
    half_size = head_size // 2
    exponent = jnp.arange(half_size, dtype=jnp.float32) * (2.0 / head_size)
    inverse = jnp.exp(-exponent * math.log(ROPE_BASE))
    angles = positions.astype(jnp.float32)[:, None] * inverse[None, :]
    return (jnp.cos(angles), jnp.sin(angles))


def rotate(values, cos_table, sin_table):
    half_size = values.shape[-1] // 2
    lower_half = values[..., :half_size]
    upper_half = values[..., half_size:]
    cos_part = cos_table[:, None, :]
    sin_part = sin_table[:, None, :]
    return jnp.concatenate(
        [
            lower_half * cos_part - upper_half * sin_part,
            upper_half * cos_part + lower_half * sin_part,
        ],
        axis=-1,
    )


def cdiv(value, step):
    return -(-value // step)


def exchange(blocks, axis, groups=None):
    return lax.all_to_all(
        blocks, axis, split_axis=0, concat_axis=0, axis_index_groups=groups, tiled=True
    )


def fold(blocks):
    return jnp.sum(blocks.astype(jnp.float32), axis=0).astype(jnp.bfloat16)


def scatter_sum(partial, batch_count, ctx_count):
    rows, columns = partial.shape
    own_rows = rows // (batch_count * ctx_count)
    pair = 2 if ctx_count % 2 == 0 else 1
    far = ctx_count // pair
    near_groups = [[f * pair + p for p in range(pair)] for f in range(far)]
    far_groups = [[f * pair + p for f in range(far)] for p in range(pair)]
    held = partial.reshape(batch_count, far, pair, own_rows, columns)
    held = jnp.transpose(held, (2, 0, 1, 3, 4))
    if pair > 1:
        held = exchange(held, "ctx", near_groups)
    held = fold(held)
    held = fold(exchange(held, "batch"))
    return jnp.sum(exchange(held, "ctx", far_groups).astype(jnp.float32), axis=0)


def attend(queries, key_rows, value_rows, allowed, score_scale):
    scores = (
        jnp.einsum("tkgd,skd->kgts", queries, key_rows, preferred_element_type=jnp.float32)
        * score_scale
    )
    exp_scores = jnp.where(allowed[None, None], jnp.exp(scores), 0.0)
    totals = jnp.sum(exp_scores, axis=-1, keepdims=True)
    prob_wire = (exp_scores / totals).astype(jnp.bfloat16)
    output = jnp.einsum("kgts,skd->tkgd", prob_wire, value_rows, preferred_element_type=jnp.float32)
    return (output.astype(jnp.bfloat16), jnp.log(totals))


def score_grads(
    queries, key_rows, value_rows, allowed, score_scale, log_totals, delta_heads, grad_rows
):
    scores = (
        jnp.einsum("tkgd,skd->kgts", queries, key_rows, preferred_element_type=jnp.float32)
        * score_scale
    )
    prob_again = jnp.where(allowed[None, None], jnp.exp(scores - log_totals), 0.0)
    grad_prob = jnp.einsum(
        "tkgd,skd->kgts", grad_rows, value_rows, preferred_element_type=jnp.float32
    )
    grad_score = (prob_again * (grad_prob - delta_heads) * score_scale).astype(jnp.bfloat16)
    return (prob_again.astype(jnp.bfloat16), grad_score)


def shards(
    inputs,
    segments,
    routes,
    cotangent,
    w_query,
    w_key,
    w_value,
    w_output,
    w_router,
    norm_attn,
    norm_moe,
    w_gate,
    w_up,
    w_down,
):
    tok_rows = inputs.shape[1]
    model_width = inputs.shape[2]
    ctx_count = lax.axis_size("ctx")
    batch_count = lax.axis_size("batch")
    ctx_index = lax.axis_index("ctx")
    batch_index = lax.axis_index("batch")
    device_count = ctx_count * batch_count
    seq_length = tok_rows * ctx_count
    groups_per = HEADS // KV_HEADS
    kv_width = KV_HEADS * HEAD_DIM
    query_width = HEADS * HEAD_DIM
    own_rows, experts = w_router.shape
    unit_count = w_gate.shape[2]
    held_experts = w_gate.shape[0]
    spread = held_experts % batch_count == 0
    slot_total = experts * CAP
    score_scale = 1.0 / math.sqrt(HEAD_DIM)
    residual_in = inputs[0].astype(jnp.float32)
    seg_local = segments[0]
    grad_wire = cotangent[0]
    grad_out = grad_wire.astype(jnp.float32)

    if spread:
        served = held_experts // batch_count
        token_axes = ("batch", "ctx")
        order = [
            (c * batch_count + b) * served + j
            for b in range(batch_count)
            for c in range(ctx_count)
            for j in range(served)
        ]
    else:
        served = held_experts
        token_axes = "ctx"
        order = list(range(experts))
    place = [order.index(e) for e in range(experts)]
    order_row = jnp.array(order, dtype=jnp.int32)
    route_mask = jnp.any(routes[0][:, :, None] == order_row[None, None, :], axis=1)
    token_row = jnp.arange(tok_rows, dtype=jnp.int32)
    before = (token_row[None, :] < token_row[:, None]).astype(jnp.bfloat16)
    turn = jnp.dot(
        before, route_mask.astype(jnp.bfloat16), preferred_element_type=jnp.float32
    ).astype(jnp.int32)
    slot_mask = route_mask[:, :, None] & (
        turn[:, :, None] == jnp.arange(CAP, dtype=jnp.int32)[None, None, :]
    )
    dispatch = slot_mask.astype(jnp.bfloat16).reshape(tok_rows, slot_total)

    def send_tokens(rows):
        picked = lax.dot_general(
            dispatch, rows, (((0,), (0,)), ((), ())), preferred_element_type=jnp.float32
        ).astype(jnp.bfloat16)
        arrived = exchange(picked.reshape(experts, CAP, model_width), token_axes)
        return arrived.reshape(-1, served, CAP, model_width)

    def return_tokens(rows):
        back = exchange(rows.reshape(experts, CAP, model_width), token_axes)
        return jnp.dot(
            dispatch, back.reshape(slot_total, model_width), preferred_element_type=jnp.float32
        )

    seg_columns = cdiv(tok_rows, own_rows)
    seg_pad = jnp.pad(seg_local, (0, seg_columns * own_rows - tok_rows))
    small_width = experts + 2 + seg_columns
    small_pad = cdiv(small_width, 128) * 128 - small_width
    dense_own = jnp.concatenate(
        [
            w_query,
            w_key,
            w_value,
            w_output,
            w_router[:, order_row] if spread else w_router,
            norm_attn[:, None],
            norm_moe[:, None],
            seg_pad.reshape(own_rows, seg_columns).astype(jnp.bfloat16),
            jnp.zeros((own_rows, small_pad), jnp.bfloat16),
        ],
        axis=1,
    )
    dense_full = lax.all_gather(dense_own, ("batch", "ctx"), axis=0, tiled=True)
    qkv_width = query_width + 2 * kv_width
    qkv_full = dense_full[:, :qkv_width]
    output_full = dense_full[:, qkv_width : qkv_width + model_width]
    small_full = dense_full[:, qkv_width + model_width :]
    router_full = small_full[:, :experts]
    gain_attn = small_full[:, experts].astype(jnp.float32)
    gain_moe = small_full[:, experts + 1].astype(jnp.float32)
    seg_devices = small_full[:, experts + 2 : small_width].reshape(batch_count, ctx_count, -1)
    seg_all = lax.dynamic_index_in_dim(
        seg_devices[:, :, :tok_rows].reshape(batch_count, seq_length),
        batch_index,
        0,
        keepdims=False,
    )

    expert_own = jnp.concatenate([w_gate, w_up, w_down], axis=2)
    if spread:
        expert_full = lax.all_to_all(
            expert_own, "batch", split_axis=0, concat_axis=1, tiled=True
        )
    else:
        expert_full = lax.all_gather(expert_own, "batch", axis=1, tiled=True)
    gate_up_full = expert_full[:, :, : 2 * unit_count]
    down_full = expert_full[:, :, 2 * unit_count :]
    grad_rows_moe = send_tokens(grad_wire)

    positions = ctx_index * tok_rows + jnp.arange(tok_rows, dtype=jnp.int32)
    cos_table, sin_table = rope_tables(positions, HEAD_DIM)
    inv_first = lax.rsqrt(jnp.mean(residual_in * residual_in, axis=-1, keepdims=True) + EPS)
    normed_attn = (residual_in * inv_first * gain_attn).astype(jnp.bfloat16)
    projected = jnp.dot(normed_attn, qkv_full, preferred_element_type=jnp.float32)
    rotated = rotate(
        projected[:, : query_width + kv_width].reshape(tok_rows, HEADS + KV_HEADS, HEAD_DIM),
        cos_table,
        sin_table,
    ).astype(jnp.bfloat16)
    query_rot = rotated[:, :HEADS]
    key_rot = rotated[:, HEADS:]
    value_rows = projected[:, query_width + kv_width :].astype(jnp.bfloat16)
    kv_all = lax.all_gather(
        jnp.concatenate([key_rot.reshape(tok_rows, kv_width), value_rows], axis=1),
        "ctx",
        axis=0,
        tiled=True,
    )
    seg_wire = seg_local.astype(jnp.bfloat16)
    key_pos = jnp.arange(seq_length, dtype=jnp.int32)
    allowed = (seg_wire[:, None] == seg_all[None, :]) & (key_pos[None, :] <= positions[:, None])
    query_groups = query_rot.reshape(tok_rows, KV_HEADS, groups_per, HEAD_DIM)
    key_heads = kv_all[:, :kv_width].reshape(seq_length, KV_HEADS, HEAD_DIM)
    value_heads = kv_all[:, kv_width:].reshape(seq_length, KV_HEADS, HEAD_DIM)
    attn_rows, log_totals = attend(query_groups, key_heads, value_heads, allowed, score_scale)
    attn_flat = attn_rows.reshape(tok_rows, query_width)
    hidden_res = residual_in + jnp.dot(attn_flat, output_full, preferred_element_type=jnp.float32)
    inv_second = lax.rsqrt(jnp.mean(hidden_res * hidden_res, axis=-1, keepdims=True) + EPS)
    normed_moe = (hidden_res * inv_second * gain_moe).astype(jnp.bfloat16)

    logits = jnp.dot(normed_moe, router_full, preferred_element_type=jnp.float32)
    route_exp = jnp.where(route_mask, jnp.exp(logits), 0.0)
    route_weights = route_exp / jnp.sum(route_exp, axis=-1, keepdims=True)
    slot_weight = jnp.sum(jnp.where(slot_mask, route_weights[:, :, None], 0.0), axis=0)
    arrived = send_tokens(normed_moe)
    weight_arrived = exchange(slot_weight, token_axes).reshape(-1, served, CAP)[..., None]

    gate_up = jnp.einsum("gesd,edf->gesf", arrived, gate_up_full, preferred_element_type=jnp.float32)
    gate_pre = gate_up[..., :unit_count]
    up_pre = gate_up[..., unit_count:]
    sigmoid_gate = jax.nn.sigmoid(gate_pre)
    silu_gate = gate_pre * sigmoid_gate
    hidden_act = (silu_gate * up_pre).astype(jnp.bfloat16)
    expert_out = jnp.einsum(
        "gesf,edf->gesd", hidden_act, down_full, preferred_element_type=jnp.float32
    )
    grad_rows_wide = grad_rows_moe.astype(jnp.float32)
    grad_dots = jnp.sum(grad_rows_wide * expert_out, axis=-1)
    dots_back = exchange(grad_dots.reshape(experts, CAP), token_axes)
    grad_slots = (weight_arrived * grad_rows_wide).astype(jnp.bfloat16)
    grad_hidden = jnp.einsum(
        "gesd,edf->gesf", grad_slots, down_full, preferred_element_type=jnp.float32
    )
    grad_gate = grad_hidden * up_pre * sigmoid_gate * (1.0 + gate_pre * (1.0 - sigmoid_gate))
    grad_up = grad_hidden * silu_gate
    grad_gate_up = jnp.concatenate([grad_gate, grad_up], axis=-1).astype(jnp.bfloat16)
    grad_expert_in = jnp.einsum(
        "gesf,edf->gesd", grad_gate_up, gate_up_full, preferred_element_type=jnp.float32
    ).astype(jnp.bfloat16)
    grad_from_experts = return_tokens(grad_expert_in)
    grad_w_gate_up = jnp.einsum(
        "gesd,gesf->edf", arrived, grad_gate_up, preferred_element_type=jnp.float32
    )
    grad_w_down = jnp.einsum(
        "gesd,gesf->edf", grad_slots, hidden_act, preferred_element_type=jnp.float32
    )
    grad_experts = jnp.concatenate([grad_w_gate_up, grad_w_down], axis=2).astype(jnp.bfloat16)
    weighted_out = (weight_arrived * expert_out).astype(jnp.bfloat16)
    if spread:
        expert_sum = lax.all_to_all(
            grad_experts, "batch", split_axis=1, concat_axis=0, tiled=True
        )
    else:
        expert_sum = lax.psum_scatter(grad_experts, "batch", scatter_dimension=1, tiled=True)
    expert_sum = expert_sum.astype(jnp.float32)
    moe_out = return_tokens(weighted_out)
    block_out = (hidden_res + moe_out).astype(jnp.bfloat16)

    grad_weights = jnp.sum(jnp.where(slot_mask, dots_back[None], 0.0), axis=-1)
    grad_chosen = route_weights * (
        grad_weights - jnp.sum(route_weights * grad_weights, axis=-1, keepdims=True)
    )
    grad_logits = grad_chosen.astype(jnp.bfloat16)
    grad_router = jnp.dot(normed_moe.T, grad_logits, preferred_element_type=jnp.float32)
    grad_normed = (
        jnp.dot(grad_logits, router_full.T, preferred_element_type=jnp.float32)
        + grad_from_experts
    )
    gained_moe = grad_normed * gain_moe
    grad_gain_moe = jnp.sum(grad_normed * hidden_res * inv_second, axis=0)
    grad_hidden_res = (
        grad_out
        + inv_second * gained_moe
        - hidden_res * inv_second**3 * jnp.mean(gained_moe * hidden_res, axis=-1, keepdims=True)
    )
    grad_attn = grad_hidden_res.astype(jnp.bfloat16)
    grad_w_output = jnp.dot(attn_flat.T, grad_attn, preferred_element_type=jnp.float32)
    tail_pad = cdiv(experts + 1, 128) * 128 - experts - 1
    first_sum = scatter_sum(
        jnp.concatenate(
            [
                grad_w_output,
                grad_router,
                grad_gain_moe[:, None],
                jnp.zeros((model_width, tail_pad), jnp.float32),
            ],
            axis=1,
        ).astype(jnp.bfloat16),
        batch_count,
        ctx_count,
    )

    grad_attn_rows = (
        jnp.dot(grad_attn, output_full.T, preferred_element_type=jnp.float32)
        .astype(jnp.bfloat16)
        .reshape(tok_rows, KV_HEADS, groups_per, HEAD_DIM)
    )
    delta_rows = jnp.sum(
        grad_attn_rows.astype(jnp.float32) * attn_rows.astype(jnp.float32), axis=-1
    )
    query_all = lax.all_gather(query_rot.reshape(tok_rows, query_width), "ctx", axis=0, tiled=True)
    grad_rows_all = lax.all_gather(
        grad_attn_rows.reshape(tok_rows, query_width), "ctx", axis=0, tiled=True
    )
    stats_all = lax.all_gather(
        jnp.concatenate(
            [
                jnp.transpose(log_totals[..., 0], (2, 0, 1)).reshape(tok_rows, HEADS),
                delta_rows.reshape(tok_rows, HEADS),
            ],
            axis=1,
        ),
        "ctx",
        axis=0,
        tiled=True,
    )
    prob_wire, grad_score = score_grads(
        query_groups,
        key_heads,
        value_heads,
        allowed,
        score_scale,
        log_totals,
        jnp.transpose(delta_rows, (1, 2, 0))[..., None],
        grad_attn_rows,
    )
    grad_query_rot = jnp.einsum(
        "kgts,skd->tkgd", grad_score, key_heads, preferred_element_type=jnp.float32
    )
    log_all = stats_all[:, :HEADS].reshape(seq_length, KV_HEADS, groups_per)
    delta_all = stats_all[:, HEADS:].reshape(seq_length, KV_HEADS, groups_per)
    query_seq = query_all.reshape(seq_length, KV_HEADS, groups_per, HEAD_DIM)
    grad_seq = grad_rows_all.reshape(seq_length, KV_HEADS, groups_per, HEAD_DIM)
    allowed_keys = (seg_all[:, None] == seg_wire[None, :]) & (
        positions[None, :] <= key_pos[:, None]
    )
    prob_keys, score_keys = score_grads(
        query_seq,
        key_rot,
        value_rows.reshape(tok_rows, KV_HEADS, HEAD_DIM),
        allowed_keys,
        score_scale,
        jnp.transpose(log_all, (1, 2, 0))[..., None],
        jnp.transpose(delta_all, (1, 2, 0))[..., None],
        grad_seq,
    )
    grad_key_own = jnp.einsum(
        "kgts,tkgd->skd", score_keys, query_seq, preferred_element_type=jnp.float32
    )
    grad_value_own = jnp.einsum(
        "kgts,tkgd->skd", prob_keys, grad_seq, preferred_element_type=jnp.float32
    )
    grad_rotated = rotate(
        jnp.concatenate(
            [grad_query_rot.reshape(tok_rows, HEADS, HEAD_DIM), grad_key_own], axis=1
        ),
        cos_table,
        -sin_table,
    )
    grad_qkv = jnp.concatenate(
        [
            grad_rotated.reshape(tok_rows, query_width + kv_width),
            grad_value_own.reshape(tok_rows, kv_width),
        ],
        axis=1,
    ).astype(jnp.bfloat16)
    grad_w_qkv = jnp.dot(normed_attn.T, grad_qkv, preferred_element_type=jnp.float32)
    grad_normed_attn = jnp.dot(grad_qkv, qkv_full.T, preferred_element_type=jnp.float32)
    gained_attn = grad_normed_attn * gain_attn
    grad_gain_attn = jnp.sum(grad_normed_attn * residual_in * inv_first, axis=0)
    grad_inputs = (
        grad_hidden_res
        + inv_first * gained_attn
        - residual_in * inv_first**3 * jnp.mean(gained_attn * residual_in, axis=-1, keepdims=True)
    )
    last_sum = scatter_sum(
        jnp.concatenate(
            [
                grad_w_qkv,
                grad_gain_attn[:, None],
                jnp.zeros((model_width, 127), jnp.float32),
            ],
            axis=1,
        ).astype(jnp.bfloat16),
        batch_count,
        ctx_count,
    )
    router_sum = first_sum[:, model_width : model_width + experts]
    if spread:
        router_sum = router_sum[:, jnp.array(place, dtype=jnp.int32)]
    return (
        block_out[None],
        grad_inputs[None],
        last_sum[:, :query_width],
        last_sum[:, query_width : query_width + kv_width],
        last_sum[:, query_width + kv_width : qkv_width],
        first_sum[:, :model_width],
        router_sum,
        last_sum[:, qkv_width],
        first_sum[:, model_width + experts],
        expert_sum[:, :, :unit_count],
        expert_sum[:, :, unit_count : 2 * unit_count],
        expert_sum[:, :, 2 * unit_count :],
    )


def solution(mesh):
    placed = (
        P("batch", "ctx", None),
        P("batch", "ctx"),
        P("batch", "ctx", None),
        P("batch", "ctx", None),
        P(("batch", "ctx"), None),
        P(("batch", "ctx"), None),
        P(("batch", "ctx"), None),
        P(("batch", "ctx"), None),
        P(("batch", "ctx"), None),
        P(("batch", "ctx")),
        P(("batch", "ctx")),
        P("ctx", "batch", None),
        P("ctx", "batch", None),
        P("ctx", "batch", None),
    )
    return jax.shard_map(
        shards,
        mesh=mesh,
        in_specs=placed,
        out_specs=(
            P("batch", "ctx", None),
            P("batch", "ctx", None),
            P(("batch", "ctx"), None),
            P(("batch", "ctx"), None),
            P(("batch", "ctx"), None),
            P(("batch", "ctx"), None),
            P(("batch", "ctx"), None),
            P(("batch", "ctx")),
            P(("batch", "ctx")),
            P("ctx", "batch", None),
            P("ctx", "batch", None),
            P("ctx", "batch", None),
        ),
        check_vma=False,
    )
```

```python
import math

import jax
import jax.numpy as jnp
from jax import lax
from jax.sharding import PartitionSpec as P

HEADS = 16
KV_HEADS = 8
HEAD_DIM = 64
CAP = 48


EPS = 1e-06
ROPE_BASE = 10000.0


def rope_tables(positions, head_size):
    half_size = head_size // 2
    exponent = jnp.arange(half_size, dtype=jnp.float32) * (2.0 / head_size)
    inverse = jnp.exp(-exponent * math.log(ROPE_BASE))
    angles = positions.astype(jnp.float32)[:, None] * inverse[None, :]
    return (jnp.cos(angles), jnp.sin(angles))


def rotate(values, cos_table, sin_table):
    half_size = values.shape[-1] // 2
    lower_half = values[..., :half_size]
    upper_half = values[..., half_size:]
    cos_part = cos_table[:, None, :]
    sin_part = sin_table[:, None, :]
    return jnp.concatenate(
        [
            lower_half * cos_part - upper_half * sin_part,
            upper_half * cos_part + lower_half * sin_part,
        ],
        axis=-1,
    )


def cdiv(value, step):
    return -(-value // step)


def exchange(blocks, axis, groups=None):
    return lax.all_to_all(
        blocks, axis, split_axis=0, concat_axis=0, axis_index_groups=groups, tiled=True
    )


def fold(blocks):
    return jnp.sum(blocks.astype(jnp.float32), axis=0).astype(jnp.bfloat16)


def scatter_sum(partial, batch_count, ctx_count):
    rows, columns = partial.shape
    own_rows = rows // (batch_count * ctx_count)
    pair = 2 if ctx_count % 2 == 0 else 1
    far = ctx_count // pair
    near_groups = [[f * pair + p for p in range(pair)] for f in range(far)]
    far_groups = [[f * pair + p for f in range(far)] for p in range(pair)]
    held = partial.reshape(pair, batch_count, far, own_rows, columns)
    if pair > 1:
        held = exchange(held, "ctx", near_groups)
    held = fold(held)
    held = fold(exchange(held, "batch"))
    return jnp.sum(exchange(held, "ctx", far_groups).astype(jnp.float32), axis=0)


def attend(queries, key_rows, value_rows, allowed, score_scale):
    scores = (
        jnp.einsum("tkgd,skd->kgts", queries, key_rows, preferred_element_type=jnp.float32)
        * score_scale
    )
    exp_scores = jnp.where(allowed[None, None], jnp.exp(scores), 0.0)
    totals = jnp.sum(exp_scores, axis=-1, keepdims=True)
    prob_wire = (exp_scores / totals).astype(jnp.bfloat16)
    output = jnp.einsum("kgts,skd->tkgd", prob_wire, value_rows, preferred_element_type=jnp.float32)
    return (output.astype(jnp.bfloat16), jnp.log(totals))


def score_grads(
    queries, key_rows, value_rows, allowed, score_scale, log_totals, delta_heads, grad_rows
):
    scores = (
        jnp.einsum("tkgd,skd->kgts", queries, key_rows, preferred_element_type=jnp.float32)
        * score_scale
    )
    prob_again = jnp.where(allowed[None, None], jnp.exp(scores - log_totals), 0.0)
    grad_prob = jnp.einsum(
        "tkgd,skd->kgts", grad_rows, value_rows, preferred_element_type=jnp.float32
    )
    grad_score = (prob_again * (grad_prob - delta_heads) * score_scale).astype(jnp.bfloat16)
    return (prob_again.astype(jnp.bfloat16), grad_score)


def shards(
    inputs,
    segments,
    routes,
    cotangent,
    w_query,
    w_key,
    w_value,
    w_output,
    w_router,
    norm_attn,
    norm_moe,
    w_gate,
    w_up,
    w_down,
):
    tok_rows = inputs.shape[1]
    model_width = inputs.shape[2]
    ctx_count = lax.axis_size("ctx")
    batch_count = lax.axis_size("batch")
    ctx_index = lax.axis_index("ctx")
    batch_index = lax.axis_index("batch")
    device_count = ctx_count * batch_count
    seq_length = tok_rows * ctx_count
    groups_per = HEADS // KV_HEADS
    kv_width = KV_HEADS * HEAD_DIM
    query_width = HEADS * HEAD_DIM
    own_rows, experts = w_router.shape
    unit_count = w_gate.shape[2]
    held_experts = w_gate.shape[0]
    spread = held_experts % batch_count == 0
    slot_total = experts * CAP
    score_scale = 1.0 / math.sqrt(HEAD_DIM)
    residual_in = inputs[0].astype(jnp.float32)
    seg_local = segments[0]
    grad_wire = cotangent[0]
    grad_out = grad_wire.astype(jnp.float32)

    if spread:
        served = held_experts // batch_count
        token_axes = ("batch", "ctx")
        order = [
            (c * batch_count + b) * served + j
            for b in range(batch_count)
            for c in range(ctx_count)
            for j in range(served)
        ]
    else:
        served = held_experts
        token_axes = "ctx"
        order = list(range(experts))
    place = [order.index(e) for e in range(experts)]
    order_row = jnp.array(order, dtype=jnp.int32)
    route_mask = jnp.any(routes[0][:, :, None] == order_row[None, None, :], axis=1)
    token_row = jnp.arange(tok_rows, dtype=jnp.int32)
    before = (token_row[None, :] < token_row[:, None]).astype(jnp.bfloat16)
    turn = jnp.dot(
        before, route_mask.astype(jnp.bfloat16), preferred_element_type=jnp.float32
    ).astype(jnp.int32)
    slot_mask = route_mask[:, :, None] & (
        turn[:, :, None] == jnp.arange(CAP, dtype=jnp.int32)[None, None, :]
    )
    dispatch = slot_mask.astype(jnp.bfloat16).reshape(tok_rows, slot_total)

    def send_tokens(rows):
        picked = lax.dot_general(
            dispatch, rows, (((0,), (0,)), ((), ())), preferred_element_type=jnp.float32
        ).astype(jnp.bfloat16)
        arrived = exchange(picked.reshape(experts, CAP, model_width), token_axes)
        return arrived.reshape(-1, served, CAP, model_width)

    def return_tokens(rows):
        back = exchange(rows.reshape(experts, CAP, model_width), token_axes)
        return jnp.dot(
            dispatch, back.reshape(slot_total, model_width), preferred_element_type=jnp.float32
        )

    pair = 2 if ctx_count % 2 == 0 else 1

    def paired(features):
        blocks = features.reshape(-1, batch_count, ctx_count // pair, pair, own_rows)
        return jnp.transpose(blocks, (0, 3, 1, 2, 4)).reshape(-1, model_width)

    seg_columns = cdiv(tok_rows, own_rows)
    seg_pad = jnp.pad(seg_local, (0, seg_columns * own_rows - tok_rows))
    small_width = experts + 2 + seg_columns
    small_pad = cdiv(small_width, 128) * 128 - small_width
    dense_own = jnp.concatenate(
        [
            w_query,
            w_key,
            w_value,
            w_output,
            w_router[:, order_row] if spread else w_router,
            norm_attn[:, None],
            norm_moe[:, None],
            seg_pad.reshape(own_rows, seg_columns).astype(jnp.bfloat16),
            jnp.zeros((own_rows, small_pad), jnp.bfloat16),
        ],
        axis=1,
    )
    dense_full = lax.all_gather(dense_own, ("batch", "ctx"), axis=0, tiled=True)
    grad_rows_moe = send_tokens(grad_wire)
    dense_full, grad_rows_moe = lax.optimization_barrier((dense_full, grad_rows_moe))
    qkv_width = query_width + 2 * kv_width
    qkv_full = dense_full[:, :qkv_width]
    output_full = dense_full[:, qkv_width : qkv_width + model_width]
    small_full = dense_full[:, qkv_width + model_width :]
    router_full = small_full[:, :experts]
    gain_attn = small_full[:, experts].astype(jnp.float32)
    gain_moe = small_full[:, experts + 1].astype(jnp.float32)
    seg_devices = small_full[:, experts + 2 : small_width].reshape(batch_count, ctx_count, -1)
    seg_all = lax.dynamic_index_in_dim(
        seg_devices[:, :, :tok_rows].reshape(batch_count, seq_length),
        batch_index,
        0,
        keepdims=False,
    )

    expert_own = jnp.concatenate([w_gate, w_up, w_down], axis=2)
    if spread:
        expert_full = lax.all_to_all(
            expert_own, "batch", split_axis=0, concat_axis=1, tiled=True
        )
    else:
        expert_full = lax.all_gather(expert_own, "batch", axis=1, tiled=True)
    gate_up_full = expert_full[:, :, : 2 * unit_count]
    down_full = expert_full[:, :, 2 * unit_count :]

    positions = ctx_index * tok_rows + jnp.arange(tok_rows, dtype=jnp.int32)
    cos_table, sin_table = rope_tables(positions, HEAD_DIM)
    inv_first = lax.rsqrt(jnp.mean(residual_in * residual_in, axis=-1, keepdims=True) + EPS)
    normed_attn = (residual_in * inv_first * gain_attn).astype(jnp.bfloat16)
    projected = jnp.dot(normed_attn, qkv_full, preferred_element_type=jnp.float32)
    rotated = rotate(
        projected[:, : query_width + kv_width].reshape(tok_rows, HEADS + KV_HEADS, HEAD_DIM),
        cos_table,
        sin_table,
    ).astype(jnp.bfloat16)
    query_rot = rotated[:, :HEADS]
    key_rot = rotated[:, HEADS:]
    value_rows = projected[:, query_width + kv_width :].astype(jnp.bfloat16)
    kv_all = lax.all_gather(
        jnp.concatenate([key_rot.reshape(tok_rows, kv_width), value_rows], axis=1),
        "ctx",
        axis=0,
        tiled=True,
    )
    seg_wire = seg_local.astype(jnp.bfloat16)
    key_pos = jnp.arange(seq_length, dtype=jnp.int32)
    allowed = (seg_wire[:, None] == seg_all[None, :]) & (key_pos[None, :] <= positions[:, None])
    query_groups = query_rot.reshape(tok_rows, KV_HEADS, groups_per, HEAD_DIM)
    key_heads = kv_all[:, :kv_width].reshape(seq_length, KV_HEADS, HEAD_DIM)
    value_heads = kv_all[:, kv_width:].reshape(seq_length, KV_HEADS, HEAD_DIM)
    attn_rows, log_totals = attend(query_groups, key_heads, value_heads, allowed, score_scale)
    attn_flat = attn_rows.reshape(tok_rows, query_width)
    hidden_res = residual_in + jnp.dot(attn_flat, output_full, preferred_element_type=jnp.float32)
    inv_second = lax.rsqrt(jnp.mean(hidden_res * hidden_res, axis=-1, keepdims=True) + EPS)
    normed_moe = (hidden_res * inv_second * gain_moe).astype(jnp.bfloat16)

    logits = jnp.dot(normed_moe, router_full, preferred_element_type=jnp.float32)
    route_exp = jnp.where(route_mask, jnp.exp(logits), 0.0)
    route_weights = route_exp / jnp.sum(route_exp, axis=-1, keepdims=True)
    slot_weight = jnp.sum(jnp.where(slot_mask, route_weights[:, :, None], 0.0), axis=0)
    arrived = send_tokens(normed_moe)
    weight_arrived = exchange(slot_weight, token_axes).reshape(-1, served, CAP)[..., None]

    gate_up = jnp.einsum("gesd,edf->gesf", arrived, gate_up_full, preferred_element_type=jnp.float32)
    gate_pre = gate_up[..., :unit_count]
    up_pre = gate_up[..., unit_count:]
    sigmoid_gate = jax.nn.sigmoid(gate_pre)
    silu_gate = gate_pre * sigmoid_gate
    hidden_act = silu_gate * up_pre
    grad_plain = jnp.einsum(
        "gesd,edf->gesf", grad_rows_moe, down_full, preferred_element_type=jnp.float32
    )
    grad_dots = jnp.sum(grad_plain * hidden_act, axis=-1)
    dots_back = exchange(grad_dots.reshape(experts, CAP), token_axes)
    hidden_weighted = (weight_arrived * hidden_act).astype(jnp.bfloat16)
    grad_hidden = weight_arrived * grad_plain
    grad_gate = grad_hidden * up_pre * sigmoid_gate * (1.0 + gate_pre * (1.0 - sigmoid_gate))
    grad_up = grad_hidden * silu_gate
    grad_gate = grad_gate.astype(jnp.bfloat16)
    grad_up = grad_up.astype(jnp.bfloat16)
    grad_expert_in = jnp.einsum(
        "gesf,edf->gesd",
        jnp.concatenate([grad_gate, grad_up], axis=-1),
        gate_up_full,
        preferred_element_type=jnp.float32,
    ).astype(jnp.bfloat16)
    grad_from_experts = return_tokens(grad_expert_in)
    grad_experts = jnp.concatenate(
        [
            jnp.einsum("gesd,gesf->edf", rows, units, preferred_element_type=jnp.float32).astype(
                jnp.bfloat16
            )
            for rows, units in (
                (arrived, grad_gate),
                (arrived, grad_up),
                (grad_rows_moe, hidden_weighted),
            )
        ],
        axis=0,
    )
    if spread:
        expert_sum = lax.all_to_all(
            grad_experts, "batch", split_axis=1, concat_axis=0, tiled=True
        )
    else:
        expert_sum = lax.psum_scatter(grad_experts, "batch", scatter_dimension=1, tiled=True)
    expert_sum = expert_sum.reshape(-1, 3, served, expert_sum.shape[1], unit_count)
    weighted_out = jnp.einsum(
        "gesf,edf->gesd", hidden_weighted, down_full, preferred_element_type=jnp.float32
    ).astype(jnp.bfloat16)
    moe_out = return_tokens(weighted_out)

    grad_weights = jnp.sum(jnp.where(slot_mask, dots_back[None], 0.0), axis=-1)
    grad_chosen = route_weights * (
        grad_weights - jnp.sum(route_weights * grad_weights, axis=-1, keepdims=True)
    )
    grad_logits = grad_chosen.astype(jnp.bfloat16)
    grad_router = jnp.dot(paired(normed_moe).T, grad_logits, preferred_element_type=jnp.float32)
    grad_normed = (
        jnp.dot(grad_logits, router_full.T, preferred_element_type=jnp.float32)
        + grad_from_experts
    )
    gained_moe = grad_normed * gain_moe
    grad_gain_moe = jnp.sum(grad_normed * hidden_res * inv_second, axis=0)
    grad_hidden_res = (
        grad_out
        + inv_second * gained_moe
        - hidden_res * inv_second**3 * jnp.mean(gained_moe * hidden_res, axis=-1, keepdims=True)
    )
    grad_attn = grad_hidden_res.astype(jnp.bfloat16)
    grad_w_output = jnp.dot(paired(attn_flat).T, grad_attn, preferred_element_type=jnp.float32)

    grad_attn_rows = (
        jnp.dot(grad_attn, output_full.T, preferred_element_type=jnp.float32)
        .astype(jnp.bfloat16)
        .reshape(tok_rows, KV_HEADS, groups_per, HEAD_DIM)
    )
    delta_rows = jnp.sum(
        grad_attn_rows.astype(jnp.float32) * attn_rows.astype(jnp.float32), axis=-1
    )
    query_all = lax.all_gather(query_rot.reshape(tok_rows, query_width), "ctx", axis=0, tiled=True)
    stats = jnp.concatenate(
        [
            jnp.transpose(log_totals[..., 0], (2, 0, 1)).reshape(tok_rows, HEADS),
            delta_rows.reshape(tok_rows, HEADS),
        ],
        axis=1,
    )
    stats_high = lax.reduce_precision(stats, 8, 7)
    stats_pieces = jnp.concatenate([stats_high, stats - stats_high], axis=1).astype(jnp.bfloat16)
    back_all = lax.all_gather(
        jnp.concatenate(
            [
                grad_attn_rows.reshape(tok_rows, query_width),
                stats_pieces,
                jnp.zeros((tok_rows, -4 * HEADS % 128), jnp.bfloat16),
            ],
            axis=1,
        ),
        "ctx",
        axis=0,
        tiled=True,
    )
    grad_rows_all = back_all[:, :query_width]
    pieces_all = back_all[:, query_width : query_width + 4 * HEADS].astype(jnp.float32)
    stats_all = pieces_all[:, : 2 * HEADS] + pieces_all[:, 2 * HEADS :]
    prob_wire, grad_score = score_grads(
        query_groups,
        key_heads,
        value_heads,
        allowed,
        score_scale,
        log_totals,
        jnp.transpose(delta_rows, (1, 2, 0))[..., None],
        grad_attn_rows,
    )
    grad_query_rot = jnp.einsum(
        "kgts,skd->tkgd", grad_score, key_heads, preferred_element_type=jnp.float32
    )
    log_all = stats_all[:, :HEADS].reshape(seq_length, KV_HEADS, groups_per)
    delta_all = stats_all[:, HEADS:].reshape(seq_length, KV_HEADS, groups_per)
    query_seq = query_all.reshape(seq_length, KV_HEADS, groups_per, HEAD_DIM)
    grad_seq = grad_rows_all.reshape(seq_length, KV_HEADS, groups_per, HEAD_DIM)
    allowed_keys = (seg_all[:, None] == seg_wire[None, :]) & (
        positions[None, :] <= key_pos[:, None]
    )
    prob_keys, score_keys = score_grads(
        query_seq,
        key_rot,
        value_rows.reshape(tok_rows, KV_HEADS, HEAD_DIM),
        allowed_keys,
        score_scale,
        jnp.transpose(log_all, (1, 2, 0))[..., None],
        jnp.transpose(delta_all, (1, 2, 0))[..., None],
        grad_seq,
    )
    grad_key_own = jnp.einsum(
        "kgts,tkgd->skd", score_keys, query_seq, preferred_element_type=jnp.float32
    )
    grad_value_own = jnp.einsum(
        "kgts,tkgd->skd", prob_keys, grad_seq, preferred_element_type=jnp.float32
    )
    grad_rotated = rotate(
        jnp.concatenate(
            [grad_query_rot.reshape(tok_rows, HEADS, HEAD_DIM), grad_key_own], axis=1
        ),
        cos_table,
        -sin_table,
    )
    grad_qkv = jnp.concatenate(
        [
            grad_rotated.reshape(tok_rows, query_width + kv_width),
            grad_value_own.reshape(tok_rows, kv_width),
        ],
        axis=1,
    ).astype(jnp.bfloat16)
    grad_qkv, moe_out = lax.optimization_barrier((grad_qkv, moe_out))
    block_out = (hidden_res + moe_out).astype(jnp.bfloat16)
    grad_w_qkv = jnp.dot(paired(normed_attn).T, grad_qkv, preferred_element_type=jnp.float32)
    grad_normed_attn = jnp.dot(grad_qkv, qkv_full.T, preferred_element_type=jnp.float32)
    gained_attn = grad_normed_attn * gain_attn
    grad_gain_attn = jnp.sum(grad_normed_attn * residual_in * inv_first, axis=0)
    grad_inputs = (
        grad_hidden_res
        + inv_first * gained_attn
        - residual_in * inv_first**3 * jnp.mean(gained_attn * residual_in, axis=-1, keepdims=True)
    )
    gains = paired(jnp.stack([grad_gain_attn, grad_gain_moe])).T
    dense_partial, expert_sum = lax.optimization_barrier(
        (jnp.concatenate(
            [
                grad_w_qkv.astype(jnp.bfloat16),
                grad_w_output.astype(jnp.bfloat16),
                grad_router.astype(jnp.bfloat16),
                gains.astype(jnp.bfloat16),
                jnp.zeros((model_width, -(experts + 2) % 128), jnp.bfloat16),
            ],
            axis=1,
        ), expert_sum)
    )
    dense_sum = scatter_sum(dense_partial, batch_count, ctx_count)
    small_sum = dense_sum[:, qkv_width + model_width :]
    router_sum = small_sum[:, :experts]
    if spread:
        router_sum = router_sum[:, jnp.array(place, dtype=jnp.int32)]

    def own_experts(kind):
        return expert_sum[:, kind].reshape(w_gate.shape).astype(jnp.float32)

    return (
        block_out[None],
        grad_inputs[None],
        dense_sum[:, :query_width],
        dense_sum[:, query_width : query_width + kv_width],
        dense_sum[:, query_width + kv_width : qkv_width],
        dense_sum[:, qkv_width : qkv_width + model_width],
        router_sum,
        small_sum[:, experts],
        small_sum[:, experts + 1],
        own_experts(0),
        own_experts(1),
        own_experts(2),
    )


def solution(mesh):
    placed = (
        P("batch", "ctx", None),
        P("batch", "ctx"),
        P("batch", "ctx", None),
        P("batch", "ctx", None),
        P(("batch", "ctx"), None),
        P(("batch", "ctx"), None),
        P(("batch", "ctx"), None),
        P(("batch", "ctx"), None),
        P(("batch", "ctx"), None),
        P(("batch", "ctx")),
        P(("batch", "ctx")),
        P("ctx", "batch", None),
        P("ctx", "batch", None),
        P("ctx", "batch", None),
    )
    return jax.shard_map(
        shards,
        mesh=mesh,
        in_specs=placed,
        out_specs=(
            P("batch", "ctx", None),
            P("batch", "ctx", None),
            P(("batch", "ctx"), None),
            P(("batch", "ctx"), None),
            P(("batch", "ctx"), None),
            P(("batch", "ctx"), None),
            P(("batch", "ctx"), None),
            P(("batch", "ctx")),
            P(("batch", "ctx")),
            P("ctx", "batch", None),
            P("ctx", "batch", None),
            P("ctx", "batch", None),
        ),
        check_vma=False,
    )
```
